32 devices in a mesh: group: 2 (over x), expert: 16 (over z, y, core).
Axes of the slice: x: 2, y: 2, z: 4, core: 2. Of those that a mesh axis runs over, the one named last changes fastest.
Arguments:
- hidden: bfloat16 [4096, 4096], P(('group', 'expert')), parts along dimension 0, may hold values from -6 to 6
- norm_gain: bfloat16 [4096], replicated, may hold values from 0.25 to 1.75
- router_weight: bfloat16 [4096, 128], replicated, may hold values from -0.03125 to 0.03125
- expert_ids: int32 [4096, 8], P(('group', 'expert')), parts along dimension 0, may hold values from 0 to 127, all different within a row; in each aligned block of 128 rows (0 to 127, 128 to 255, ...) at most 16 rows name the same one
- gate_weight: bfloat16 [16, 4096, 384], P('expert'), may hold values from -0.09375 to 0.09375
- up_weight: bfloat16 [16, 4096, 384], P('expert'), may hold values from -0.09375 to 0.09375
- down_weight: bfloat16 [16, 384, 4096], P('expert'), may hold values from -0.625 to 0.625
Outputs:
- moe_out: bfloat16 [4096, 4096], P(('group', 'expert')), parts along dimension 0
The draws below stay inside these ranges and needn't reach their ends.
There are 2 independent parts, one for each index of `group`. The reference program is written for one: setup_inputs(seed, part) draws one part's arguments, and reference() takes and returns one part's arrays. A program takes and returns all parts, laid end to end along the dimension named above; an argument that names none is the same for every part. Nothing has to cross between parts.
Inputs may be any that keep to these rules, and one draw needn't show every extreme that they name: `expert_ids`: each row names 8 different experts; in each aligned block of 128 rows (the rows of one device) no expert is named by more than 16 rows.
All inputs are finite; a program needn't handle non-finite values.
Results may differ from the reference program's by a relative error of at most 0.0077.
Values may be sent and summed in bfloat16 or wider, within the bound.
A program may use at most 128 MiB of HBM per device.

```python
import math
import jax
import jax.numpy as jnp
import numpy as np
from jax import lax

D = 4096
FF = 1536
EXPERTS = 128
TOP = 8
TOK_DEV = 128
SPLIT = 4
SLICE = 384
E_FLIGHT = 4
CAP = 16
TOKENS = 2048
N_EXPERT = 16


def levels(stream_key, extent, pieces, least, largest):
    factor_of, own = 1.0, jax.random.fold_in(stream_key, 6)
    for position, blocks in pieces:
        steps = jnp.exp(jax.random.uniform(jax.random.fold_in(own, position), (blocks,), jnp.float32, least / len(pieces), largest / len(pieces)))
        factor_of = factor_of * jnp.repeat(steps, extent[position] // blocks).reshape([-1 if axis == position else 1 for axis in range(len(extent))])
    return factor_of


def shared_out(key, own, number, rows, count, top, reach, lean):
    ranking = jax.random.permutation(key, count)
    packed, usual = load_shares(count, rows * top, reach, lean, True), load_shares(count, rows * top, reach, lean, False)
    places = jnp.arange(count)

    def named(lengths, turn):
        used = int((lengths > 0).sum())
        fixed = max(1, used // 4)
        shifted = fixed + (places - fixed + turn * (used - fixed)) % max(1, count - fixed)
        return jnp.zeros((count,), jnp.int32).at[ranking[jnp.where(places < fixed, places, shifted)]].set(jnp.asarray(lengths, jnp.int32))

    lengths = jnp.where(number % 4 == 0, named(packed, number // 4), named(usual, number - number // 4 - 1))
    mixed = jax.random.permutation(jax.random.fold_in(own, 3), count)
    donor, sink = mixed[0:count // 2 * 2:2], mixed[1:count // 2 * 2:2]
    room = jnp.minimum(lengths[donor] - 1, reach - lengths[sink]) // 2
    room = jnp.where((donor == ranking[0]) | (sink == ranking[0]) | (lengths[sink] == 0), 0, jnp.maximum(room, 0))
    shifted = jax.random.randint(jax.random.fold_in(own, 4), (count // 2,), 0, 1 << 20) % (room + 1)
    lengths = lengths.at[donor].add(-shifted).at[sink].add(shifted)
    labels = jnp.searchsorted(jnp.cumsum(lengths), jnp.arange(rows * top), side="right").astype(jnp.int32)
    table = labels.reshape(top, rows).T
    table = table[jax.random.permutation(jax.random.fold_in(own, 1), rows)]
    turn = jax.random.randint(jax.random.fold_in(own, 2), (rows, 1), 0, top)
    return jnp.take_along_axis(table, (jnp.arange(top)[None, :] + turn) % top, axis=1)


def load_shares(number_of, total, most, skew, full):
    loads = [(1 << 20) // math.isqrt(rank ** skew) + 1 for rank in range(1, number_of + 1)]
    largest = most if full else min(most, max(-(-total // number_of), total * loads[0] // sum(loads)))
    least = 1 if total - largest >= number_of - 1 else 0
    holding, rest = [largest] + [least] * (number_of - 1), total - largest - least * (number_of - 1)
    while rest > 0:
        free = [i for i in range(1, number_of) if holding[i] < largest] or [i for i in range(1, number_of) if holding[i] < most]
        whole, remaining = sum([loads[i] for i in free]), rest
        for i in free:
            more = min(most - holding[i], max(1, remaining * loads[i] // whole), rest)
            holding[i] = holding[i] + more
            rest = rest - more
    return np.array(holding)


def noise(key, dims, width, limit, cuts=(), kind=jnp.bfloat16):
    drawn = jax.random.normal(key, dims, jnp.float32) * width
    if len(cuts) > 0:
        drawn = levels(key, dims, cuts, -0.22, 0.18) * drawn
    return jnp.clip(drawn, min=-limit, max=limit).astype(kind)


def setup_inputs(seed: int = 0, part: int = 0) -> dict:
    keys = jax.random.split(jax.random.key(seed), 8)
    part_splits = jax.random.split(jax.random.fold_in(keys[7], part), 8)
    hidden = noise(part_splits[0], (TOKENS, D), 1.0, 6.0, ((0, 16),))
    norm_gain = jnp.clip(1.0 + 0.15 * jax.random.normal(keys[1], (D,), jnp.float32), 0.25, 1.75).astype(jnp.bfloat16)
    router_weight = noise(keys[2], (D, EXPERTS), (8 * D) ** -0.5, 0.03125)
    expert_ids_keys = jax.random.split(jax.random.fold_in(part_splits[3], 1), TOKENS // TOK_DEV)
    expert_ids_turns = jax.random.permutation(jax.random.fold_in(part_splits[3], 3), TOKENS // TOK_DEV)
    expert_ids = jax.vmap(lambda own, number: shared_out(jax.random.fold_in(part_splits[3], 2), own, number, TOK_DEV, EXPERTS, TOP, CAP, 2))(expert_ids_keys, expert_ids_turns).reshape((TOKENS, TOP))
    gate_weight = noise(keys[4], (N_EXPERT, D, SLICE), D ** -0.5, 0.09375, ((0, 16),))
    up_weight = noise(keys[5], (N_EXPERT, D, SLICE), D ** -0.5, 0.09375, ((0, 16),))
    down_weight = noise(keys[6], (N_EXPERT, SLICE, D), (FF // 16) ** -0.5, 0.625, ((0, 16),))
    return {"hidden": hidden, "norm_gain": norm_gain, "router_weight": router_weight, "expert_ids": expert_ids, "gate_weight": gate_weight, "up_weight": up_weight, "down_weight": down_weight}


def reference(hidden, norm_gain, router_weight, expert_ids, gate_weight, up_weight, down_weight):
    widened = hidden.astype(jnp.float32)
    inv_rms = lax.rsqrt(lax.optimization_barrier(jnp.mean(widened * widened, axis=-1, keepdims=True)) + 1e-06)
    normed = (widened * inv_rms * norm_gain.astype(jnp.float32)).astype(jnp.bfloat16)
    logits = jnp.dot(normed, router_weight, preferred_element_type=jnp.float32)
    router_probs = jax.nn.softmax(logits, axis=-1)
    picked = jnp.take_along_axis(router_probs, expert_ids, axis=1)
    gate_share = picked / lax.optimization_barrier(jnp.sum(picked, axis=1, keepdims=True))

    def one_expert(expert, running):
        summed = jnp.zeros(hidden.shape, jnp.float32)
        for member in range(SPLIT):
            shard_row = member * E_FLIGHT + expert
            gate_mat = lax.dynamic_index_in_dim(gate_weight, shard_row, 0, keepdims=False)
            up_mat = lax.dynamic_index_in_dim(up_weight, shard_row, 0, keepdims=False)
            down_mat = lax.dynamic_index_in_dim(down_weight, shard_row, 0, keepdims=False)
            gate_act = jnp.dot(normed, gate_mat, preferred_element_type=jnp.float32)
            up_act = jnp.dot(normed, up_mat, preferred_element_type=jnp.float32)
            hidden_act = (jax.nn.silu(gate_act) * up_act).astype(jnp.bfloat16)
            partial_value = jnp.dot(hidden_act, down_mat, preferred_element_type=jnp.float32).astype(jnp.bfloat16)
            summed = summed + lax.optimization_barrier(partial_value).astype(jnp.float32)
        expert_out = lax.optimization_barrier(summed.astype(jnp.bfloat16)).astype(jnp.float32)
        weight = lax.optimization_barrier(jnp.sum(jnp.where(expert_ids == expert, gate_share, jnp.zeros_like(gate_share)), axis=1))
        return running + weight[:, None] * expert_out
    running = lax.fori_loop(0, E_FLIGHT, one_expert, jnp.zeros(hidden.shape, jnp.float32))
    return running.astype(jnp.bfloat16)
```

```python
import functools

import jax
import jax.numpy as jnp
from jax import lax
from jax.experimental import pallas as pl
from jax.experimental.pallas import tpu as pltpu
from jax.sharding import PartitionSpec as P

SPLIT = 4
CAP = 16
F32 = jnp.float32
BF16 = jnp.bfloat16


def route_kernel(flight, hidden_ref, gain_ref, router_ref, ids_ref, out_ref, hi_ref, lo_ref):
    rows = hidden_ref.shape[0]
    experts = router_ref.shape[1]
    cols = flight * CAP
    widened = hidden_ref[...].astype(F32)
    inv_rms = lax.rsqrt(jnp.mean(widened * widened, axis=-1, keepdims=True) + 1e-06)
    normed = (widened * inv_rms * gain_ref[...].astype(F32)).astype(BF16)
    logits = jnp.dot(normed, router_ref[...], preferred_element_type=F32)
    shifted = jnp.exp(logits - jnp.max(logits, axis=-1, keepdims=True))
    probs = shifted / jnp.sum(shifted, axis=-1, keepdims=True)
    ids = ids_ref[...]
    expert = lax.broadcasted_iota(jnp.int32, (rows, experts), 1)
    chosen = jnp.zeros((rows, experts), F32)
    for k in range(ids.shape[1]):
        chosen = jnp.where(ids[:, k : k + 1] == expert, 1.0, chosen)
    picked = probs * chosen
    share = picked / jnp.sum(picked, axis=-1, keepdims=True)
    chosen_b = chosen.astype(BF16)
    earlier = lax.broadcasted_iota(jnp.int32, (rows, rows), 1) < lax.broadcasted_iota(
        jnp.int32, (rows, rows), 0
    )
    slot = jnp.dot(jnp.where(earlier, 1.0, 0.0).astype(BF16), chosen_b, preferred_element_type=F32)
    spread = (
        lax.broadcasted_iota(jnp.int32, (experts, cols), 1) // CAP
        == lax.broadcasted_iota(jnp.int32, (experts, cols), 0)
    )
    spread = jnp.where(spread, 1.0, 0.0).astype(BF16)
    slot_of = jnp.dot(slot.astype(BF16), spread, preferred_element_type=F32)
    live_of = jnp.dot(chosen_b, spread, preferred_element_type=F32)
    share_hi = share.astype(BF16)
    share_lo = (share - share_hi.astype(F32)).astype(BF16)
    hi_of = jnp.dot(share_hi, spread, preferred_element_type=F32)
    lo_of = jnp.dot(share_lo, spread, preferred_element_type=F32)
    place = (lax.broadcasted_iota(jnp.int32, (rows, cols), 1) % CAP).astype(F32)
    select = (live_of > 0.5) & (slot_of == place)
    hi_ref[...] = jnp.where(select, hi_of, 0.0).astype(BF16)
    lo_ref[...] = jnp.where(select, lo_of, 0.0).astype(BF16)
    dispatch = jnp.where(select, 1.0, 0.0).astype(BF16)
    out_ref[...] = lax.dot_general(
        dispatch, normed, (((0,), (0,)), ((), ())), preferred_element_type=F32
    ).astype(BF16)


def expert_kernel(
    flight,
    out_ref,
    hi_ref,
    lo_ref,
    gate_hbm,
    up_hbm,
    down_hbm,
    moe_ref,
    gate_v,
    up_v,
    down_v,
    act_v,
    x_v,
    p_v,
    r_v,
    res_v,
    w_sem,
    own_sem,
    p1_send,
    p1_recv,
    ag_send,
    ag_recv,
    rs_send,
    rs_recv,
    ret_send,
    ret_recv,
):
    dev = lax.axis_index("expert")
    m = dev // flight
    e = dev % flight
    last = SPLIT - 1
    width = out_ref.shape[1]
    tile = min(512, width)

    weights = [
        pltpu.make_async_copy(gate_hbm.at[0], gate_v, w_sem.at[0]),
        pltpu.make_async_copy(up_hbm.at[0], up_v, w_sem.at[1]),
        pltpu.make_async_copy(down_hbm.at[0], down_v, w_sem.at[2]),
    ]
    for copy in weights:
        copy.start()

    def band(c):
        return pl.ds(pl.multiple_of(c * CAP, CAP), CAP)

    def remote(src, dst, ssem, rsem, target):
        return pltpu.make_async_remote_copy(
            src_ref=src,
            dst_ref=dst,
            send_sem=ssem,
            recv_sem=rsem,
            device_id={"expert": target},
            device_id_type=pl.DeviceIdType.MESH,
        )

    def mate(j):
        return (e + j) % flight

    barrier = pltpu.get_barrier_semaphore()

    def greet(target):
        pl.semaphore_signal(
            barrier, inc=1, device_id={"expert": target}, device_id_type=pl.DeviceIdType.MESH
        )

    @pl.loop(1, flight)
    def _(j):
        greet(m * flight + mate(j))

    @pl.when(m > 0)
    def _():
        greet(dev - flight)

    @pl.when(m < last)
    def _():
        greet(dev + flight)

    pl.semaphore_wait(
        barrier, flight - 1 + jnp.where(m > 0, 1, 0) + jnp.where(m < last, 1, 0)
    )

    def first(j):
        c = mate(j)
        return remote(
            out_ref.at[band(c)],
            x_v.at[m, band(e)],
            p1_send.at[c],
            p1_recv.at[e],
            m * flight + c,
        )

    def first_arrival(c):
        return remote(out_ref.at[band(c)], x_v.at[m, band(c)], p1_send.at[c], p1_recv.at[c], dev)

    own = pltpu.make_async_copy(out_ref.at[band(e)], x_v.at[m, band(e)], own_sem.at[0])
    own.start()

    @pl.loop(1, flight)
    def _(j):
        first(j).start()

    def pass_on(s, c, up):
        target = dev + flight if up else dev - flight
        return remote(
            x_v.at[s, band(c)],
            x_v.at[s, band(c)],
            ag_send.at[1 if up else 0, s, c],
            ag_recv.at[s, c],
            target,
        )

    def spread(s, c):
        @pl.when((m < last) & (s <= m))
        def _():
            pass_on(s, c, True).start()

        @pl.when((m > 0) & (s >= m))
        def _():
            pass_on(s, c, False).start()

    own.wait()
    spread(m, e)

    @pl.loop(1, flight)
    def _(j):
        c = mate(flight - j)
        first_arrival(c).wait_recv()
        spread(m, c)

    for copy in weights:
        copy.wait()

    def give(s, c, up):
        if up:
            target = dev + flight
            slot = jnp.where(s == m + 1, SPLIT, s)
        else:
            target = dev - flight
            slot = s
        return remote(
            p_v.at[s, band(c)], r_v.at[slot, band(c)], rs_send.at[s, c], rs_recv.at[slot, c], target
        )

    def taken(slot, c):
        return remote(
            r_v.at[slot, band(c)], r_v.at[slot, band(c)], rs_send.at[0, c], rs_recv.at[slot, c], dev
        )

    def compute(s):
        rows = x_v[s]
        gate = jnp.dot(rows, gate_v[...], preferred_element_type=F32)
        up = jnp.dot(rows, up_v[...], preferred_element_type=F32)
        act_v[...] = (jax.nn.silu(gate) * up).astype(BF16)

        @pl.loop(0, width // tile)
        def _(i):
            at = pl.ds(pl.multiple_of(i * tile, tile), tile)
            p_v[s, :, at] = jnp.dot(
                act_v[...], down_v[:, at], preferred_element_type=F32
            ).astype(BF16)

    @pl.loop(0, SPLIT)
    def _(t):
        @pl.loop(0, 2)
        def _(d):
            s = jnp.where(d == 0, m - t, m + t)

            @pl.when((t > 0) & (s >= 0) & (s <= last))
            def _():
                @pl.loop(0, flight)
                def _(c):
                    pass_on(s, c, True).wait_recv()
                    spread(s, c)

        @pl.loop(0, 2)
        def _(d):
            s = jnp.where(d == 0, m - t, m + t)

            @pl.when((s >= 0) & (s <= last) & ((t > 0) | (d == 0)))
            def _():
                compute(s)

                @pl.when((s < m) & (m == last))
                def _():
                    @pl.loop(0, flight)
                    def _(c):
                        give(s, c, False).start()

                @pl.when((s > m) & (m == 0))
                def _():
                    @pl.loop(0, flight)
                    def _(c):
                        give(s, c, True).start()

    def add(s, slot, c):
        taken(slot, c).wait_recv()
        p_v[s, band(c), :] = (
            p_v[s, band(c), :].astype(F32) + r_v[slot, band(c), :].astype(F32)
        ).astype(BF16)

    @pl.loop(3, 2 * last)
    def _(due):
        fall = 2 * last - m - due
        rise = due - m

        @pl.when((fall >= 0) & (fall < m) & (m < last))
        def _():
            @pl.loop(0, flight)
            def _(c):
                add(fall, fall, c)
                give(fall, c, False).start()

        @pl.when((rise <= last) & (rise > m) & (m > 0))
        def _():
            @pl.loop(0, flight)
            def _(c):
                add(rise, rise, c)
                give(rise, c, True).start()

    def back(c):
        return remote(
            p_v.at[m, band(c)],
            res_v.at[band(e)],
            ret_send.at[c],
            ret_recv.at[e],
            m * flight + c,
        )

    def back_arrival(c):
        return remote(p_v.at[m, band(c)], res_v.at[band(c)], ret_send.at[c], ret_recv.at[c], dev)

    @pl.loop(0, flight)
    def _(j):
        c = mate(j)

        @pl.when(m < last)
        def _():
            taken(m, c).wait_recv()

        @pl.when(m > 0)
        def _():
            taken(SPLIT, c).wait_recv()

        total = p_v[m, band(c), :].astype(F32)
        above = r_v[jnp.where(m < last, m, SPLIT), band(c), :].astype(F32)
        below = r_v[jnp.where(m > 0, SPLIT, m), band(c), :].astype(F32)
        both = jnp.where((m > 0) & (m < last), 1.0, 0.0)
        total = (total + above + both * below).astype(BF16)
        p_v[m, band(c), :] = total

        @pl.when(j > 0)
        def _():
            back(c).start()

    keep = pltpu.make_async_copy(p_v.at[m, band(e)], res_v.at[band(e)], own_sem.at[1])
    keep.start()
    keep.wait()

    @pl.loop(1, flight)
    def _(j):
        back_arrival(mate(j)).wait_recv()

    @pl.loop(0, width // tile)
    def _(i):
        at = pl.ds(pl.multiple_of(i * tile, tile), tile)
        results = res_v[:, at]
        moe_ref[:, at] = (
            jnp.dot(hi_ref[...], results, preferred_element_type=F32)
            + jnp.dot(lo_ref[...], results, preferred_element_type=F32)
        ).astype(BF16)

    @pl.loop(1, flight)
    def _(j):
        first(j).wait_send()
        back(mate(j)).wait_send()

    @pl.loop(0, SPLIT)
    def _(s):
        @pl.loop(0, flight)
        def _(c):
            @pl.when((m < last) & (s <= m))
            def _():
                pass_on(s, c, True).wait_send()

            @pl.when((m > 0) & (s >= m))
            def _():
                pass_on(s, c, False).wait_send()

            @pl.when(s != m)
            def _():
                give(s, c, False).wait_send()


def shards(flight, hidden, norm_gain, router_weight, expert_ids, gate_weight, up_weight, down_weight):
    rows, width = hidden.shape
    cols = flight * CAP
    slice_width = gate_weight.shape[2]
    vmem = pl.BlockSpec(memory_space=pltpu.VMEM)
    hbm = pl.BlockSpec(memory_space=pl.ANY)
    outgoing, hi, lo = pl.pallas_call(
        functools.partial(route_kernel, flight),
        out_shape=(
            jax.ShapeDtypeStruct((cols, width), BF16),
            jax.ShapeDtypeStruct((rows, cols), BF16),
            jax.ShapeDtypeStruct((rows, cols), BF16),
        ),
        in_specs=[vmem] * 4,
        out_specs=(vmem,) * 3,
    )(hidden, norm_gain.reshape(1, width), router_weight, expert_ids)
    dma = pltpu.SemaphoreType.DMA
    return pl.pallas_call(
        functools.partial(expert_kernel, flight),
        out_shape=jax.ShapeDtypeStruct((rows, width), BF16),
        in_specs=[vmem] * 3 + [hbm] * 3,
        out_specs=vmem,
        scratch_shapes=[
            pltpu.VMEM((width, slice_width), BF16),
            pltpu.VMEM((width, slice_width), BF16),
            pltpu.VMEM((slice_width, width), BF16),
            pltpu.VMEM((cols, slice_width), BF16),
            pltpu.VMEM((SPLIT, cols, width), BF16),
            pltpu.VMEM((SPLIT, cols, width), BF16),
            pltpu.VMEM((SPLIT + 1, cols, width), BF16),
            pltpu.VMEM((cols, width), BF16),
            dma((3,)),
            dma((2,)),
            dma((flight,)),
            dma((flight,)),
            dma((2, SPLIT, flight)),
            dma((SPLIT, flight)),
            dma((SPLIT, flight)),
            dma((SPLIT + 1, flight)),
            dma((flight,)),
            dma((flight,)),
        ],
        compiler_params=pltpu.CompilerParams(collective_id=0, has_side_effects=True),
    )(outgoing, hi, lo, gate_weight, up_weight, down_weight)


def solution(mesh):
    flight = mesh.shape["expert"] // SPLIT
    in_specs = (
        P(("group", "expert"), None),
        P(),
        P(),
        P(("group", "expert"), None),
        P("expert", None, None),
        P("expert", None, None),
        P("expert", None, None),
    )
    out_specs = P(("group", "expert"), None)
    return jax.shard_map(
        functools.partial(shards, flight),
        mesh=mesh,
        in_specs=in_specs,
        out_specs=out_specs,
        check_vma=False,
    )
```

```python
import functools

import jax
import jax.numpy as jnp
from jax import lax
from jax.experimental import pallas as pl
from jax.experimental.pallas import tpu as pltpu
from jax.sharding import PartitionSpec as P

SPLIT = 4
CAP = 16
F32 = jnp.float32
BF16 = jnp.bfloat16


def route_kernel(flight, hidden_ref, gain_ref, router_ref, ids_ref, out_ref, hi_ref, lo_ref):
    rows = hidden_ref.shape[0]
    experts = router_ref.shape[1]
    cols = flight * CAP
    widened = hidden_ref[...].astype(F32)
    inv_rms = lax.rsqrt(jnp.mean(widened * widened, axis=-1, keepdims=True) + 1e-06)
    normed = (widened * inv_rms * gain_ref[...].astype(F32)[None, :]).astype(BF16)
    logits = jnp.dot(normed, router_ref[...], preferred_element_type=F32)
    shifted = jnp.exp(logits - jnp.max(logits, axis=-1, keepdims=True))
    probs = shifted / jnp.sum(shifted, axis=-1, keepdims=True)
    ids = ids_ref[...]
    expert = lax.broadcasted_iota(jnp.int32, (experts, rows), 0)
    chosen = jnp.zeros((experts, rows), F32)
    for k in range(ids.shape[0]):
        chosen = jnp.where(ids[k : k + 1, :] == expert, 1.0, chosen)
    chosen = chosen.T
    picked = probs * chosen
    share = picked / jnp.sum(picked, axis=-1, keepdims=True)
    chosen_b = chosen.astype(BF16)
    earlier = lax.broadcasted_iota(jnp.int32, (rows, rows), 1) < lax.broadcasted_iota(
        jnp.int32, (rows, rows), 0
    )
    slot = jnp.dot(jnp.where(earlier, 1.0, 0.0).astype(BF16), chosen_b, preferred_element_type=F32)
    spread = (
        lax.broadcasted_iota(jnp.int32, (experts, cols), 1) // CAP
        == lax.broadcasted_iota(jnp.int32, (experts, cols), 0)
    )
    spread = jnp.where(spread, 1.0, 0.0).astype(BF16)
    slot_of = jnp.dot(slot.astype(BF16), spread, preferred_element_type=F32)
    live_of = jnp.dot(chosen_b, spread, preferred_element_type=F32)
    share_hi = share.astype(BF16)
    share_lo = (share - share_hi.astype(F32)).astype(BF16)
    hi_of = jnp.dot(share_hi, spread, preferred_element_type=F32)
    lo_of = jnp.dot(share_lo, spread, preferred_element_type=F32)
    place = (lax.broadcasted_iota(jnp.int32, (rows, cols), 1) % CAP).astype(F32)
    select = (live_of > 0.5) & (slot_of == place)
    hi_ref[...] = jnp.where(select, hi_of, 0.0).astype(BF16)
    lo_ref[...] = jnp.where(select, lo_of, 0.0).astype(BF16)
    dispatch = jnp.where(select, 1.0, 0.0).astype(BF16)
    out_ref[...] = lax.dot_general(
        dispatch, normed, (((0,), (0,)), ((), ())), preferred_element_type=F32
    ).astype(BF16)


def expert_kernel(
    flight,
    out_ref,
    hi_ref,
    lo_ref,
    gate_hbm,
    up_hbm,
    down_hbm,
    moe_ref,
    gate_v,
    up_v,
    down_v,
    act_v,
    x_v,
    p_v,
    r_v,
    res_v,
    w_sem,
    own_sem,
    p1_send,
    p1_recv,
    ag_send,
    ag_recv,
    rs_send,
    rs_recv,
    ret_send,
    ret_recv,
):
    dev = lax.axis_index("expert")
    m = dev // flight
    e = dev % flight
    last = SPLIT - 1
    width = out_ref.shape[1]
    tile = min(512, width)

    weights = [
        pltpu.make_async_copy(gate_hbm.at[0], gate_v, w_sem.at[0]),
        pltpu.make_async_copy(up_hbm.at[0], up_v, w_sem.at[1]),
        pltpu.make_async_copy(down_hbm.at[0], down_v, w_sem.at[2]),
    ]
    for copy in weights:
        copy.start()

    def band(c):
        return pl.ds(pl.multiple_of(c * CAP, CAP), CAP)

    def remote(src, dst, ssem, rsem, target):
        return pltpu.make_async_remote_copy(
            src_ref=src,
            dst_ref=dst,
            send_sem=ssem,
            recv_sem=rsem,
            device_id={"expert": target},
            device_id_type=pl.DeviceIdType.MESH,
        )

    def mate(j):
        return (e + j) % flight

    barrier = pltpu.get_barrier_semaphore()

    def greet(target):
        pl.semaphore_signal(
            barrier, inc=1, device_id={"expert": target}, device_id_type=pl.DeviceIdType.MESH
        )

    @pl.loop(1, flight)
    def _(j):
        greet(m * flight + mate(j))

    @pl.when(m > 0)
    def _():
        greet(dev - flight)

    @pl.when(m < last)
    def _():
        greet(dev + flight)

    pl.semaphore_wait(
        barrier, flight - 1 + jnp.where(m > 0, 1, 0) + jnp.where(m < last, 1, 0)
    )

    def first(j):
        c = mate(j)
        return remote(
            out_ref.at[band(c)],
            x_v.at[m, band(j)],
            p1_send.at[j],
            p1_recv.at[j],
            m * flight + c,
        )

    def first_arrival(j):
        return remote(out_ref.at[band(j)], x_v.at[m, band(j)], p1_send.at[j], p1_recv.at[j], dev)

    own = pltpu.make_async_copy(out_ref.at[band(e)], x_v.at[m, band(0)], own_sem.at[0])
    own.start()

    @pl.loop(1, flight)
    def _(j):
        first(j).start()

    def pass_on(s, c, up):
        target = dev + flight if up else dev - flight
        return remote(
            x_v.at[s, band(c)],
            x_v.at[s, band(c)],
            ag_send.at[1 if up else 0, s, c],
            ag_recv.at[s, c],
            target,
        )

    def spread(s, c):
        @pl.when((m < last) & (s <= m))
        def _():
            pass_on(s, c, True).start()

        @pl.when((m > 0) & (s >= m))
        def _():
            pass_on(s, c, False).start()

    own.wait()
    spread(m, 0)

    @pl.loop(1, flight)
    def _(j):
        first_arrival(j).wait_recv()
        spread(m, j)

    for copy in weights:
        copy.wait()

    def give(s, c, up):
        if up:
            target = dev + flight
            slot = jnp.where(s == m + 1, SPLIT, s)
        else:
            target = dev - flight
            slot = s
        return remote(
            p_v.at[s, band(c)], r_v.at[slot, band(c)], rs_send.at[s, c], rs_recv.at[slot, c], target
        )

    def taken(slot, c):
        return remote(
            r_v.at[slot, band(c)], r_v.at[slot, band(c)], rs_send.at[0, c], rs_recv.at[slot, c], dev
        )

    def compute(s, start, count):
        here = pl.ds(start, count)
        rows = x_v[s, here, :]
        gate = jnp.dot(rows, gate_v[...], preferred_element_type=F32)
        up = jnp.dot(rows, up_v[...], preferred_element_type=F32)
        act_v[here, :] = (jax.nn.silu(gate) * up).astype(BF16)

        @pl.loop(0, width // tile)
        def _(i):
            at = pl.ds(pl.multiple_of(i * tile, tile), tile)
            p_v[s, here, at] = jnp.dot(
                act_v[here, :], down_v[:, at], preferred_element_type=F32
            ).astype(BF16)

    def arrive(s, begin, end):
        @pl.loop(begin, end)
        def _(c):
            pass_on(s, c, True).wait_recv()
            spread(s, c)

    def begin_sums(s, begin, end):
        @pl.when((s < m) & (m == last))
        def _():
            @pl.loop(begin, end)
            def _(c):
                give(s, c, False).start()

        @pl.when((s > m) & (m == 0))
        def _():
            @pl.loop(begin, end)
            def _(c):
                give(s, c, True).start()

    @pl.loop(0, last)
    def _(t):
        @pl.loop(0, 2)
        def _(d):
            s = jnp.where(d == 0, m - t, m + t)

            @pl.when((t > 0) & (s >= 0) & (s <= last))
            def _():
                arrive(s, 0, flight)

        @pl.loop(0, 2)
        def _(d):
            s = jnp.where(d == 0, m - t, m + t)

            @pl.when((s >= 0) & (s <= last) & ((t > 0) | (d == 0)))
            def _():
                compute(s, 0, flight * CAP)
                begin_sums(s, 0, flight)

    pieces = 2 if flight % 2 == 0 else 1
    step = flight // pieces

    @pl.when((m == 0) | (m == last))
    def _():
        far = last - m

        @pl.loop(0, pieces)
        def _(h):
            arrive(far, h * step, (h + 1) * step)
            compute(far, pl.multiple_of(h * step * CAP, step * CAP), step * CAP)
            begin_sums(far, h * step, (h + 1) * step)

    def add(s, slot, c):
        taken(slot, c).wait_recv()
        p_v[s, band(c), :] = (
            p_v[s, band(c), :].astype(F32) + r_v[slot, band(c), :].astype(F32)
        ).astype(BF16)

    @pl.loop(3, 2 * last)
    def _(due):
        fall = 2 * last - m - due
        rise = due - m

        @pl.when((fall >= 0) & (fall < m) & (m < last))
        def _():
            @pl.loop(0, flight)
            def _(c):
                add(fall, fall, c)
                give(fall, c, False).start()

        @pl.when((rise <= last) & (rise > m) & (m > 0))
        def _():
            @pl.loop(0, flight)
            def _(c):
                add(rise, rise, c)
                give(rise, c, True).start()

    def back(j):
        return remote(
            p_v.at[m, band(j)],
            res_v.at[band(e)],
            ret_send.at[j],
            ret_recv.at[e],
            m * flight + mate(flight - j),
        )

    def back_arrival(c):
        return remote(p_v.at[m, band(c)], res_v.at[band(c)], ret_send.at[c], ret_recv.at[c], dev)

    @pl.loop(0, flight)
    def _(c):
        @pl.when(m < last)
        def _():
            taken(m, c).wait_recv()

        @pl.when(m > 0)
        def _():
            taken(SPLIT, c).wait_recv()

        total = p_v[m, band(c), :].astype(F32)
        above = r_v[jnp.where(m < last, m, SPLIT), band(c), :].astype(F32)
        below = r_v[jnp.where(m > 0, SPLIT, m), band(c), :].astype(F32)
        both = jnp.where((m > 0) & (m < last), 1.0, 0.0)
        total = (total + above + both * below).astype(BF16)
        p_v[m, band(c), :] = total

        @pl.when(c > 0)
        def _():
            back(c).start()

    keep = pltpu.make_async_copy(p_v.at[m, band(0)], res_v.at[band(e)], own_sem.at[1])
    keep.start()
    keep.wait()

    @pl.loop(1, flight)
    def _(j):
        back_arrival(mate(j)).wait_recv()

    @pl.loop(0, width // tile)
    def _(i):
        at = pl.ds(pl.multiple_of(i * tile, tile), tile)
        results = res_v[:, at]
        moe_ref[:, at] = (
            jnp.dot(hi_ref[...], results, preferred_element_type=F32)
            + jnp.dot(lo_ref[...], results, preferred_element_type=F32)
        ).astype(BF16)

    @pl.loop(1, flight)
    def _(j):
        first(j).wait_send()
        back(j).wait_send()

    @pl.loop(0, SPLIT)
    def _(s):
        @pl.loop(0, flight)
        def _(c):
            @pl.when((m < last) & (s <= m))
            def _():
                pass_on(s, c, True).wait_send()

            @pl.when((m > 0) & (s >= m))
            def _():
                pass_on(s, c, False).wait_send()

            @pl.when(s != m)
            def _():
                give(s, c, False).wait_send()


def shards(flight, hidden, norm_gain, router_weight, expert_ids, gate_weight, up_weight, down_weight):
    rows, width = hidden.shape
    cols = flight * CAP
    slice_width = gate_weight.shape[2]
    vmem = pl.BlockSpec(memory_space=pltpu.VMEM)
    hbm = pl.BlockSpec(memory_space=pl.ANY)
    outgoing, hi, lo = pl.pallas_call(
        functools.partial(route_kernel, flight),
        out_shape=(
            jax.ShapeDtypeStruct((cols, width), BF16),
            jax.ShapeDtypeStruct((rows, cols), BF16),
            jax.ShapeDtypeStruct((rows, cols), BF16),
        ),
        in_specs=[vmem] * 4,
        out_specs=(vmem,) * 3,
    )(hidden, norm_gain, router_weight, expert_ids.T)
    dma = pltpu.SemaphoreType.DMA
    return pl.pallas_call(
        functools.partial(expert_kernel, flight),
        out_shape=jax.ShapeDtypeStruct((rows, width), BF16),
        in_specs=[vmem] * 3 + [hbm] * 3,
        out_specs=vmem,
        scratch_shapes=[
            pltpu.VMEM((width, slice_width), BF16),
            pltpu.VMEM((width, slice_width), BF16),
            pltpu.VMEM((slice_width, width), BF16),
            pltpu.VMEM((cols, slice_width), BF16),
            pltpu.VMEM((SPLIT, cols, width), BF16),
            pltpu.VMEM((SPLIT, cols, width), BF16),
            pltpu.VMEM((SPLIT + 1, cols, width), BF16),
            pltpu.VMEM((cols, width), BF16),
            dma((3,)),
            dma((2,)),
            dma((flight,)),
            dma((flight,)),
            dma((2, SPLIT, flight)),
            dma((SPLIT, flight)),
            dma((SPLIT, flight)),
            dma((SPLIT + 1, flight)),
            dma((flight,)),
            dma((flight,)),
        ],
        compiler_params=pltpu.CompilerParams(collective_id=0, has_side_effects=True),
    )(outgoing, hi, lo, gate_weight, up_weight, down_weight)


def solution(mesh):
    flight = mesh.shape["expert"] // SPLIT
    in_specs = (
        P(("group", "expert"), None),
        P(),
        P(),
        P(("group", "expert"), None),
        P("expert", None, None),
        P("expert", None, None),
        P("expert", None, None),
    )
    out_specs = P(("group", "expert"), None)
    return jax.shard_map(
        functools.partial(shards, flight),
        mesh=mesh,
        in_specs=in_specs,
        out_specs=out_specs,
        check_vma=False,
    )
```
